32 devices in a mesh: chan: 4 (over y, x), space: 8 (over z, core).
Axes of the slice: x: 2, y: 2, z: 4, core: 2. Of those that a mesh axis runs over, the one named last changes fastest.
Arguments:
- volume: bfloat16 [32, 16, 256, 128], P('space', None, 'chan'), may hold values from -6 to 6
- kernel: bfloat16 [27, 256, 256], P(None, 'chan'), may hold values from -0.078125 to 0.078125
- bias: float32 [256], P('chan'), may hold values from -3 to 3
- cotangent: bfloat16 [32, 16, 256, 128], P('space', None, 'chan'), may hold values from -6 to 6
Outputs:
- output: bfloat16 [32, 16, 256, 128], P('space', None, 'chan')
- input_grad: bfloat16 [32, 16, 256, 128], P('space', None, 'chan')
- weight_grad: float32 [27, 256, 256], P(None, 'chan')
The draws below stay inside these ranges and needn't reach their ends.
All inputs are finite; a program needn't handle non-finite values.
Results may differ from the reference program's by a relative error of at most 0.0049.
Values may be sent and summed in bfloat16 or wider, within the bound.
A program may use at most 128 MiB of HBM per device.

```python
import math
import jax
import jax.numpy as jnp
from jax import lax

CIN = 256
COUT = 256
TAPS = 27
NX = 32
NY = 16
NZ = 128


def block_scale(own_key, extent, shards, least, largest):
    gain, own = 1.0, jax.random.fold_in(own_key, 6)
    for dim, blocks in shards:
        draws = jnp.exp(jax.random.uniform(jax.random.fold_in(own, dim), (blocks,), jnp.float32, least / len(shards), largest / len(shards)))
        gain = gain * jnp.repeat(draws, extent[dim] // blocks).reshape([-1 if axis == dim else 1 for axis in range(len(extent))])
    return gain


def noise(stream_key, extent, width, bound, shards=(), held_as=jnp.bfloat16):
    drawn = width * jax.random.normal(stream_key, extent, jnp.float32)
    if shards:
        drawn = drawn * block_scale(stream_key, extent, shards, -0.22, 0.18)
    return jnp.clip(drawn, -bound, bound).astype(held_as)


def setup_inputs(seed: int = 0) -> dict:
    streams_of = jax.random.split(jax.random.key(seed), 5)
    return {
        "volume": noise(streams_of[0], (NX, NY, CIN, NZ), 1.0, 6.0, ((0, 8), (2, 4))),
        "kernel": noise(streams_of[1], (TAPS, COUT, CIN), (TAPS * CIN) ** -0.5, 0.078125, ((1, 4),)),
        "bias": noise(streams_of[2], (COUT,), 0.5, 3.0, ((0, 4),), jnp.float32),
        "cotangent": noise(streams_of[3], (NX, NY, COUT, NZ), 1.0, 6.0, ((0, 8), (2, 4))),
    }


def tap_list():
    return [(first, second, third) for first in range(3) for second in range(3) for third in range(3)]

def reference(volume, kernel, bias, cotangent):
    volume_last = jnp.transpose(volume, (0, 1, 3, 2))
    cotangent_last = jnp.transpose(cotangent, (0, 1, 3, 2))
    size_x, size_y, size_z, chans_in = volume_last.shape
    chans_out = kernel.shape[1]
    cells = size_x * size_y * size_z
    kernel_f = jnp.transpose(kernel.astype(jnp.float32), (0, 2, 1))
    padded = jnp.pad(volume_last.astype(jnp.float32), ((1, 1), (1, 1), (1, 1), (0, 0)))
    accum = jnp.zeros((cells, chans_out), jnp.float32)
    for index_tap, (first, second, third) in enumerate(tap_list()):
        slab = padded[first:first + size_x, second:second + size_y, third:third + size_z, :].reshape(cells, chans_in)
        accum = accum + jnp.dot(slab, kernel_f[index_tap], precision=lax.Precision.HIGHEST, preferred_element_type=jnp.float32)
    pre = accum + bias.astype(jnp.float32)
    sigmoid_pre = jax.nn.sigmoid(pre)
    output = (pre * sigmoid_pre).astype(jnp.bfloat16).reshape(size_x, size_y, size_z, chans_out)
    grad_pre = (cotangent_last.reshape(cells, chans_out).astype(jnp.float32) * sigmoid_pre * (1.0 + pre * (1.0 - sigmoid_pre))).astype(jnp.bfloat16)
    grad_f = grad_pre.astype(jnp.float32)
    parts = []
    for index_tap, (first, second, third) in enumerate(tap_list()):
        slab = padded[first:first + size_x, second:second + size_y, third:third + size_z, :].reshape(cells, chans_in)
        parts.append(jnp.dot(grad_f.T, slab, precision=lax.Precision.HIGHEST, preferred_element_type=jnp.float32))
    weight_grad = jnp.stack(parts) / math.sqrt(cells)
    grad_padded = jnp.pad(grad_f.reshape(size_x, size_y, size_z, chans_out), ((1, 1), (1, 1), (1, 1), (0, 0)))
    back = jnp.zeros((cells, chans_in), jnp.float32)
    for index_tap, (first, second, third) in enumerate(tap_list()):
        slab = grad_padded[2 - first:2 - first + size_x, 2 - second:2 - second + size_y, 2 - third:2 - third + size_z, :].reshape(cells, chans_out)
        back = back + jnp.dot(slab, kernel_f[index_tap].T, precision=lax.Precision.HIGHEST, preferred_element_type=jnp.float32)
    input_grad = back.astype(jnp.bfloat16).reshape(size_x, size_y, size_z, chans_in)
    return (jnp.transpose(output, (0, 1, 3, 2)), jnp.transpose(input_grad, (0, 1, 3, 2)), weight_grad)
```

```python
import functools
import math

import jax
import jax.numpy as jnp
from jax import lax
from jax.experimental import pallas as pl
from jax.experimental.pallas import tpu as pltpu
from jax.sharding import PartitionSpec as P

F32 = jnp.float32
BF16 = jnp.bfloat16
VMEM_LIMIT = 60 * 1024 * 1024


def shifted(rows, amount):
    size_z = rows.shape[1]
    lane = lax.broadcasted_iota(jnp.int32, rows.shape, 1)
    edge = 0 if amount == 1 else size_z - 1
    return jnp.where(lane == edge, 0.0, pltpu.roll(rows, amount % size_z, 1))


def lay_out(lo_ref, mid_ref, hi_ref, planes):
    size_x, size_y, chans, size_z = mid_ref.shape
    edge = jnp.zeros(((size_x + 2) * chans, size_z), BF16)
    planes[:, 0:size_z] = edge
    planes[:, (size_y + 1) * size_z : (size_y + 2) * size_z] = edge
    for y in range(size_y):
        lanes = slice((y + 1) * size_z, (y + 2) * size_z)
        planes[0:chans, lanes] = lo_ref[0, y]
        planes[(size_x + 1) * chans : (size_x + 2) * chans, lanes] = hi_ref[0, y]

        def put(x, _, y=y, lanes=lanes):
            planes[pl.ds((x + 1) * chans, chans), lanes] = mid_ref[x, y]
            return 0

        lax.fori_loop(0, size_x, put, 0)


def conv_rows(planes, w_ref, chans, size_z, x, y, count):
    total = None
    for dy in range(3):
        lanes = pl.ds(pl.multiple_of((y + dy) * size_z, size_z), count * size_z)
        cells = planes[pl.ds(pl.multiple_of(x * chans, chans), 3 * chans), lanes]
        part = jnp.dot(w_ref[dy], cells, preferred_element_type=F32)
        total = part if total is None else total + part
    return total


def tap_sum(total, outs, size_z, row):
    lanes = slice(row * size_z, (row + 1) * size_z)
    return (
        total[outs : 2 * outs, lanes]
        + shifted(total[0:outs, lanes], 1)
        + shifted(total[2 * outs : 3 * outs, lanes], -1)
    )


def forward_kernel(lo_ref, mid_ref, hi_ref, w_ref, bias_ref, cot_ref, out_ref, grad_ref, three_ref, planes):
    size_x, size_y, chans, size_z = mid_ref.shape
    outs = cot_ref.shape[2]
    lay_out(lo_ref, mid_ref, hi_ref, planes)
    count = 2

    def step(index, _):
        x = index // (size_y // count)
        y = (index % (size_y // count)) * count
        total = conv_rows(planes, w_ref, chans, size_z, x, y, count)
        for row in range(count):
            pre = tap_sum(total, outs, size_z, row) + bias_ref[...]
            sig = jax.nn.sigmoid(pre)
            out_ref[x, y + row] = (pre * sig).astype(BF16)
            grad = cot_ref[x, y + row].astype(F32) * sig * (1.0 + pre * (1.0 - sig))
            held = grad.astype(BF16)
            grad_ref[x, y + row] = held
            grad = held.astype(F32)
            lanes = pl.ds(pl.multiple_of((y + row) * size_z, size_z), size_z)
            three_ref[x, 0:outs, lanes] = shifted(grad, -1).astype(BF16)
            three_ref[x, outs : 2 * outs, lanes] = held
            three_ref[x, 2 * outs : 3 * outs, lanes] = shifted(grad, 1).astype(BF16)
        return 0

    lax.fori_loop(0, size_x * size_y // count, step, 0)


def weight_kernel(three_ref, planes, acc_ref):
    size_x, _, cells = three_ref.shape
    wide = acc_ref.shape[2]
    chans = wide // 3
    size_z = (planes.shape[1] - cells) // 2
    acc_ref[...] = jnp.zeros_like(acc_ref)

    def step(x, _):
        for dy in range(3):
            cube = planes[pl.ds(pl.multiple_of(x * chans, chans), wide), dy * size_z : dy * size_z + cells]
            acc_ref[dy] += lax.dot_general(
                three_ref[x], cube, (((1,), (1,)), ((), ())), preferred_element_type=F32
            )
        return 0

    lax.fori_loop(0, size_x, step, 0)


def input_kernel(lo_ref, mid_ref, hi_ref, w_ref, out_ref, planes):
    size_x, size_y, chans, size_z = mid_ref.shape
    outs = out_ref.shape[2]
    lay_out(lo_ref, mid_ref, hi_ref, planes)
    count = 2

    def step(index, _):
        x = index // (size_y // count)
        y = (index % (size_y // count)) * count
        total = conv_rows(planes, w_ref, chans, size_z, x, y, count)
        for row in range(count):
            out_ref[x, y + row] = tap_sum(total, outs, size_z, row).astype(BF16)
        return 0

    lax.fori_loop(0, size_x * size_y // count, step, 0)


def call(kernel, args, outs, scratch, flops):
    whole = pl.BlockSpec(memory_space=pltpu.VMEM)
    size = sum(a.size * a.dtype.itemsize for a in args)
    return pl.pallas_call(
        kernel,
        out_shape=outs,
        in_specs=[whole] * len(args),
        out_specs=jax.tree.map(lambda _: whole, outs),
        scratch_shapes=scratch,
        compiler_params=pltpu.CompilerParams(vmem_limit_bytes=VMEM_LIMIT),
        cost_estimate=pl.CostEstimate(flops=flops, bytes_accessed=size, transcendentals=0),
    )(*args)


def with_neighbours(cells):
    count = lax.axis_size("space")
    up = [(i, i + 1) for i in range(count - 1)]
    down = [(i + 1, i) for i in range(count - 1)]
    lo = lax.ppermute(cells[-1:], "space", up)
    hi = lax.ppermute(cells[:1], "space", down)
    return lo, cells, hi


def on_device(volume, kernel, bias, cotangent):
    size_x, size_y, chans_local, size_z = volume.shape
    taps, outs, chans = kernel.shape
    shape = jax.ShapeDtypeStruct
    flops = 2 * size_x * size_y * size_z * taps * outs * chans
    cube = kernel.reshape(3, 3, 3, outs, chans)
    w_forward = cube.transpose(1, 2, 3, 0, 4).reshape(3, 3 * outs, 3 * chans)
    turned = lax.all_to_all(kernel, "chan", split_axis=2, concat_axis=1, tiled=True)
    all_outs, ins = turned.shape[1], turned.shape[2]
    turned = turned.reshape(3, 3, 3, all_outs, ins)[::-1, ::-1, ::-1]
    w_input = turned.transpose(1, 2, 4, 0, 3).reshape(3, 3 * ins, 3 * all_outs)
    column = jnp.broadcast_to(bias.reshape(outs, 1), (outs, size_z))

    padded = (size_y + 2) * size_z
    gathered = lax.all_gather(volume, "chan", axis=2, tiled=True)
    output, grad_pre, three, planes = call(
        forward_kernel,
        (*with_neighbours(gathered), w_forward, column, cotangent),
        (
            shape(cotangent.shape, BF16),
            shape(cotangent.shape, BF16),
            shape((size_x, 3 * outs, size_y * size_z), BF16),
            shape(((size_x + 2) * chans, padded), BF16),
        ),
        [],
        flops,
    )
    grads = lax.all_gather(grad_pre, "chan", axis=2, tiled=True)
    partial = call(weight_kernel, (three, planes), shape((3, 3 * outs, 3 * chans), F32), [], flops)
    summed = lax.psum(partial, "space") / math.sqrt(size_x * size_y * size_z * lax.axis_size("space"))
    weight_grad = summed.reshape(3, 3, outs, 3, chans).transpose(3, 0, 1, 2, 4).reshape(taps, outs, chans)
    input_grad = call(
        input_kernel,
        (*with_neighbours(grads), w_input),
        shape(volume.shape, BF16),
        [pltpu.VMEM(((size_x + 2) * all_outs, padded), BF16)],
        flops,
    )
    return output, input_grad, weight_grad


def solution(mesh):
    return jax.shard_map(
        on_device,
        mesh=mesh,
        in_specs=(
            P("space", None, "chan", None),
            P(None, "chan", None),
            P("chan"),
            P("space", None, "chan", None),
        ),
        out_specs=(
            P("space", None, "chan", None),
            P("space", None, "chan", None),
            P(None, "chan", None),
        ),
        check_vma=False,
    )
```

```python
import functools
import math

import jax
import jax.numpy as jnp
from jax import lax
from jax.experimental import pallas as pl
from jax.experimental.pallas import tpu as pltpu
from jax.sharding import PartitionSpec as P

F32 = jnp.float32
BF16 = jnp.bfloat16
VMEM_LIMIT = 60 * 1024 * 1024


def shifted(rows, amount):
    size_z = rows.shape[1]
    lane = lax.broadcasted_iota(jnp.int32, rows.shape, 1)
    edge = 0 if amount == 1 else size_z - 1
    return jnp.where(lane == edge, 0.0, pltpu.roll(rows, amount % size_z, 1))


class Gather:
    def __init__(self, source, planes, local_sem, send_sem, recv_sem, halo_send, halo_recv, peers):
        self.source, self.planes = source, planes
        self.local_sem, self.send_sem, self.recv_sem = local_sem, send_sem, recv_sem
        self.halo_send, self.halo_recv = halo_send, halo_recv
        self.size_x, self.size_y, self.part, self.size_z = source.shape
        self.peers = peers
        self.me = lax.axis_index("chan")
        self.slab = lax.axis_index("space")
        self.slabs = lax.axis_size("space")
        self.chans = self.part * peers
        self.has_lo, self.has_hi = self.slab > 0, self.slab < self.slabs - 1
        self.order = [1] + ([self.size_x] if self.size_x > 1 else []) + list(range(2, self.size_x))
        me = self.me
        if peers == 4:
            across = me // 2 * 2 + (1 - me % 2)
            along = (1 - me // 2) * 2 + me % 2
            self.owners = [me, across, along, 3 - me]
            self.near = [1, 2]
        else:
            self.owners = [(me + r) % peers for r in range(peers)]
            self.near = list(range(1, peers))

    def block(self, q, owner):
        rows = pl.ds(pl.multiple_of(q * self.chans + owner * self.part, self.part), self.part)
        return self.planes.at[rows, self.size_z : (self.size_y + 1) * self.size_z]

    def back(self, slot):
        return slot if self.peers == 4 else self.peers - slot

    def chan_copy(self, q, slot_held, toward, slot_there):
        return pltpu.make_async_remote_copy(
            src_ref=self.block(q, self.owners[slot_held]),
            dst_ref=self.block(q, self.owners[slot_held]),
            send_sem=self.send_sem.at[q, slot_there],
            recv_sem=self.recv_sem.at[q, slot_there],
            device_id=(self.me, self.slab) if toward is None else (self.owners[toward], self.slab),
            device_id_type=pl.DeviceIdType.MESH,
        )

    def arrived(self, q, slot):
        pltpu.make_async_remote_copy(
            src_ref=self.block(q, self.owners[slot]),
            dst_ref=self.block(q, self.owners[slot]),
            send_sem=self.send_sem.at[q, slot],
            recv_sem=self.recv_sem.at[q, slot],
            device_id=(self.owners[1], self.slab),
            device_id_type=pl.DeviceIdType.MESH,
        ).wait_recv()

    def halo_copy(self, slot, up):
        mine, theirs = (self.size_x, 0) if up else (1, self.size_x + 1)
        return pltpu.make_async_remote_copy(
            src_ref=self.block(mine, self.owners[slot]),
            dst_ref=self.block(theirs, self.owners[slot]),
            send_sem=self.halo_send.at[int(up), slot],
            recv_sem=self.halo_recv.at[int(up), slot],
            device_id=(self.me, self.slab + 1 if up else self.slab - 1),
            device_id_type=pl.DeviceIdType.MESH,
        )

    def halo_pass(self, q, slot):
        if q == self.size_x:

            @pl.when(self.has_hi)
            def _():
                self.halo_copy(slot, True).start()

        if q == 1:

            @pl.when(self.has_lo)
            def _():
                self.halo_copy(slot, False).start()

    def local_copy(self, q, y):
        rows = pl.ds(pl.multiple_of(q * self.chans + self.me * self.part, self.part), self.part)
        lanes = pl.ds(pl.multiple_of((y + 1) * self.size_z, self.size_z), self.size_z)
        return pltpu.make_async_copy(
            self.source.at[q - 1, y], self.planes.at[rows, lanes], self.local_sem.at[q]
        )

    def begin(self):
        for q in self.order:

            def put(y, _, q=q):
                self.local_copy(q, y).start()
                return 0

            lax.fori_loop(0, self.size_y, put, 0)
        barrier = pltpu.get_barrier_semaphore()
        for slot in range(1, self.peers):
            pl.semaphore_signal(
                barrier, inc=1, device_id=(self.owners[slot], self.slab), device_id_type=pl.DeviceIdType.MESH
            )
        for step in (1, self.slabs - 1):
            beside = (self.slab + step) % self.slabs
            pl.semaphore_signal(
                barrier, inc=1, device_id=(self.me, beside), device_id_type=pl.DeviceIdType.MESH
            )

        edge = jnp.zeros((self.planes.shape[0], self.size_z), BF16)
        self.planes[:, 0 : self.size_z] = edge
        self.planes[:, (self.size_y + 1) * self.size_z : (self.size_y + 2) * self.size_z] = edge
        cells = slice(self.size_z, (self.size_y + 1) * self.size_z)
        blank = jnp.zeros((self.chans, self.size_y * self.size_z), BF16)

        @pl.when(jnp.logical_not(self.has_lo))
        def _():
            self.planes[0 : self.chans, cells] = blank

        @pl.when(jnp.logical_not(self.has_hi))
        def _():
            self.planes[(self.size_x + 1) * self.chans : (self.size_x + 2) * self.chans, cells] = blank

        pl.semaphore_wait(barrier, self.peers + 1)

        for q in self.order:

            def done(y, _, q=q):
                self.local_copy(q, y).wait()
                return 0

            lax.fori_loop(0, self.size_y, done, 0)
            for slot in self.near:
                self.chan_copy(q, 0, slot, self.back(slot)).start()
            self.halo_pass(q, 0)

    def relay(self, stage, q, slot):
        return self.peers == 4 and slot == (1 if stage % 2 else 2)

    def take_near(self, stage):
        q = self.order[stage]
        for slot in self.near:
            self.arrived(q, slot)
            if self.relay(stage, q, slot):
                self.chan_copy(q, slot, 3 - slot, 3).start()
            self.halo_pass(q, slot)

    def take_far(self, stage):
        q = self.order[stage]
        if self.peers == 4:
            self.arrived(q, 3)
            self.halo_pass(q, 3)

    def take_halo(self, up):
        @pl.when(self.has_lo if up else self.has_hi)
        def _():
            for slot in range(self.peers):
                mine, theirs = (self.size_x, 0) if up else (1, self.size_x + 1)
                pltpu.make_async_remote_copy(
                    src_ref=self.block(mine, self.owners[slot]),
                    dst_ref=self.block(theirs, self.owners[slot]),
                    send_sem=self.halo_send.at[int(up), slot],
                    recv_sem=self.halo_recv.at[int(up), slot],
                    device_id=(self.me, self.slab - 1 if up else self.slab + 1),
                    device_id_type=pl.DeviceIdType.MESH,
                ).wait_recv()

    def finish(self):
        for stage, q in enumerate(self.order):
            for slot in self.near:
                self.chan_copy(q, 0, slot, self.back(slot)).wait_send()
                if self.relay(stage, q, slot):
                    self.chan_copy(q, slot, 3 - slot, 3).wait_send()
        for up, there in ((True, self.has_hi), (False, self.has_lo)):

            @pl.when(there)
            def _(up=up):
                for slot in range(self.peers):
                    self.halo_copy(slot, up).wait_send()


def add_plane(planes, w_ref, acc, q, started, chans, size_y, size_z):
    size_x, rows, _ = acc.shape
    taps = [dx for dx in range(3) if 0 <= q - dx < size_x]
    first, last = taps[0], taps[-1] + 1
    count = 2

    def step(index, _):
        y = index * count
        total = None
        for dy in range(3):
            lanes = pl.ds(pl.multiple_of((y + dy) * size_z, size_z), count * size_z)
            part = jnp.dot(
                w_ref[dy, first * rows : last * rows],
                planes[q * chans : (q + 1) * chans, lanes],
                preferred_element_type=F32,
            )
            total = part if total is None else total + part
        lanes = pl.ds(pl.multiple_of(y * size_z, size_z), count * size_z)
        for dx in taps:
            part = total[(dx - first) * rows : (dx - first + 1) * rows]
            if q - dx in started:
                acc[q - dx, :, lanes] += part
            else:
                acc[q - dx, :, lanes] = part
        return 0

    lax.fori_loop(0, size_y // count, step, 0)
    started.update(q - dx for dx in taps)


def tap_sum(acc, x, outs, lanes):
    return (
        acc[x, outs : 2 * outs, lanes]
        + shifted(acc[x, 0:outs, lanes], 1)
        + shifted(acc[x, 2 * outs : 3 * outs, lanes], -1)
    )


def conv(gather, w_ref, acc, finish_plane, aside):
    size_x, chans, size_y, size_z = gather.size_x, gather.chans, gather.size_y, gather.size_z
    started, count, left = set(), {x: 3 for x in range(size_x)}, list(aside)

    def plane(q):
        add_plane(gather.planes, w_ref, acc, q, started, chans, size_y, size_z)
        for dx in range(3):
            if q - dx in count:
                count[q - dx] -= 1
                if count[q - dx] == 0:
                    finish_plane(q - dx)

    gather.begin()
    stages = len(gather.order)
    for stage in range(stages):
        if left:
            left.pop(0)()
        gather.take_near(stage)
        if stage:
            gather.take_far(stage - 1)
            plane(gather.order[stage - 1])
    gather.take_halo(True)
    plane(0)
    gather.take_halo(False)
    plane(size_x + 1)
    gather.take_far(stages - 1)
    plane(gather.order[-1])
    gather.finish()


def forward_kernel(peers, vol_ref, w_ref, bias_ref, cot_ref, out_ref, grad_ref, sum_ref, planes, acc, three, *sems):
    gather = Gather(vol_ref, planes, *sems, peers)
    size_x, size_y, outs, size_z = cot_ref.shape

    def finish_plane(x):
        def step(y, _):
            lanes = pl.ds(pl.multiple_of(y * size_z, size_z), size_z)
            pre = tap_sum(acc, x, outs, lanes) + bias_ref[...]
            sig = jax.nn.sigmoid(pre)
            out_ref[x, y] = (pre * sig).astype(BF16)
            grad = cot_ref[x, y].astype(F32) * sig * (1.0 + pre * (1.0 - sig))
            held = grad.astype(BF16)
            grad_ref[x, y] = held
            grad = held.astype(F32)
            three[x, 0:outs, lanes] = shifted(grad, -1).astype(BF16)
            three[x, outs : 2 * outs, lanes] = held
            three[x, 2 * outs : 3 * outs, lanes] = shifted(grad, 1).astype(BF16)
            return 0

        lax.fori_loop(0, size_y, step, 0)

    conv(gather, w_ref, acc, finish_plane, ())
    sum_ref[...] = jnp.zeros_like(sum_ref)
    chans, cells = gather.chans, size_y * size_z

    def step(x, _):
        for dy in range(3):
            cube = planes[pl.ds(pl.multiple_of(x * chans, chans), 3 * chans), dy * size_z : dy * size_z + cells]
            sum_ref[dy] += lax.dot_general(
                three[x], cube, (((1,), (1,)), ((), ())), preferred_element_type=F32
            )
        return 0

    lax.fori_loop(0, size_x, step, 0)


def input_kernel(peers, grad_ref, w_ref, out_ref, planes, acc, *sems):
    gather = Gather(grad_ref, planes, *sems, peers)
    size_x, size_y, outs, size_z = out_ref.shape

    def finish_plane(x):
        def step(y, _):
            lanes = pl.ds(pl.multiple_of(y * size_z, size_z), size_z)
            out_ref[x, y] = tap_sum(acc, x, outs, lanes).astype(BF16)
            return 0

        lax.fori_loop(0, size_y, step, 0)

    conv(gather, w_ref, acc, finish_plane, ())


def call(kernel, args, outs, extra, rows, flops, identity):
    whole = pl.BlockSpec(memory_space=pltpu.VMEM)
    peers = lax.axis_size("chan")
    size_x, size_y, part, size_z = args[0].shape
    planes = size_x + 2
    size = sum(a.size * a.dtype.itemsize for a in args)
    return pl.pallas_call(
        functools.partial(kernel, peers),
        out_shape=outs,
        in_specs=[pl.BlockSpec(memory_space=pl.ANY)] + [whole] * (len(args) - 1),
        out_specs=jax.tree.map(lambda _: whole, outs),
        scratch_shapes=[
            pltpu.VMEM((planes * part * peers, (size_y + 2) * size_z), BF16),
            pltpu.VMEM((size_x, rows, size_y * size_z), F32),
            *extra,
            pltpu.SemaphoreType.DMA((planes,)),
            pltpu.SemaphoreType.DMA((planes, peers)),
            pltpu.SemaphoreType.DMA((planes, peers)),
            pltpu.SemaphoreType.DMA((2, peers)),
            pltpu.SemaphoreType.DMA((2, peers)),
        ],
        compiler_params=pltpu.CompilerParams(
            vmem_limit_bytes=VMEM_LIMIT, collective_id=identity, has_side_effects=True
        ),
        cost_estimate=pl.CostEstimate(flops=flops, bytes_accessed=size, transcendentals=0),
    )(*args)


def on_device(volume, kernel, bias, cotangent):
    size_x, size_y, chans_local, size_z = volume.shape
    taps, outs, chans = kernel.shape
    shape = jax.ShapeDtypeStruct
    flops = 2 * size_x * size_y * size_z * taps * outs * chans
    cube = kernel.reshape(3, 3, 3, outs, chans)
    w_forward = cube.transpose(1, 0, 2, 3, 4).reshape(3, 9 * outs, chans)
    turned = lax.all_to_all(kernel, "chan", split_axis=2, concat_axis=1, tiled=True)
    all_outs, ins = turned.shape[1], turned.shape[2]
    turned = turned.reshape(3, 3, 3, all_outs, ins)[::-1, ::-1, ::-1]
    w_input = turned.transpose(1, 0, 2, 4, 3).reshape(3, 9 * ins, all_outs)
    column = jnp.broadcast_to(bias.reshape(outs, 1), (outs, size_z))

    output, grad_pre, partial = call(
        forward_kernel,
        (volume, w_forward, column, cotangent),
        (
            shape(cotangent.shape, BF16),
            shape(cotangent.shape, BF16),
            shape((3, 3 * outs, 3 * chans), F32),
        ),
        [pltpu.VMEM((size_x, 3 * outs, size_y * size_z), BF16)],
        3 * outs,
        2 * flops,
        0,
    )
    summed = lax.psum(partial, "space") / math.sqrt(size_x * size_y * size_z * lax.axis_size("space"))
    weight_grad = summed.reshape(3, 3, outs, 3, chans).transpose(3, 0, 1, 2, 4).reshape(taps, outs, chans)
    input_grad = call(input_kernel, (grad_pre, w_input), shape(volume.shape, BF16), [], 3 * ins, flops, 1)
    return output, input_grad, weight_grad


def solution(mesh):
    return jax.shard_map(
        on_device,
        mesh=mesh,
        in_specs=(
            P("space", None, "chan", None),
            P(None, "chan", None),
            P("chan"),
            P("space", None, "chan", None),
        ),
        out_specs=(
            P("space", None, "chan", None),
            P("space", None, "chan", None),
            P(None, "chan", None),
        ),
        check_vma=False,
    )
```

```python
import functools
import math

import jax
import jax.numpy as jnp
from jax import lax
from jax.experimental import pallas as pl
from jax.experimental.pallas import tpu as pltpu
from jax.sharding import PartitionSpec as P

F32 = jnp.float32
BF16 = jnp.bfloat16
VMEM_LIMIT = 60 * 1024 * 1024


def shifted(rows, amount):
    size_z = rows.shape[1]
    lane = lax.broadcasted_iota(jnp.int32, rows.shape, 1)
    edge = 0 if amount == 1 else size_z - 1
    return jnp.where(lane == edge, 0.0, pltpu.roll(rows, amount % size_z, 1))


class Gather:
    def __init__(self, source, planes, local_sem, send_sem, recv_sem, halo_send, halo_recv, peers):
        self.source, self.planes = source, planes
        self.local_sem, self.send_sem, self.recv_sem = local_sem, send_sem, recv_sem
        self.halo_send, self.halo_recv = halo_send, halo_recv
        self.size_x, self.size_y, self.part, self.size_z = source.shape
        self.peers = peers
        self.me = lax.axis_index("chan")
        self.slab = lax.axis_index("space")
        self.slabs = lax.axis_size("space")
        self.chans = self.part * peers
        self.has_lo, self.has_hi = self.slab > 0, self.slab < self.slabs - 1
        self.order = [1] + ([self.size_x] if self.size_x > 1 else []) + list(range(2, self.size_x))
        me = self.me
        if peers == 4:
            across = me // 2 * 2 + (1 - me % 2)
            along = (1 - me // 2) * 2 + me % 2
            self.owners = [me, across, along, 3 - me]
            self.near = [1, 2]
        else:
            self.owners = [(me + r) % peers for r in range(peers)]
            self.near = list(range(1, peers))

    def block(self, q, owner):
        rows = pl.ds(pl.multiple_of(q * self.chans + owner * self.part, self.part), self.part)
        return self.planes.at[rows, self.size_z : (self.size_y + 1) * self.size_z]

    def back(self, slot):
        return slot if self.peers == 4 else self.peers - slot

    def chan_copy(self, q, slot_held, toward, slot_there):
        return pltpu.make_async_remote_copy(
            src_ref=self.block(q, self.owners[slot_held]),
            dst_ref=self.block(q, self.owners[slot_held]),
            send_sem=self.send_sem.at[q, slot_there],
            recv_sem=self.recv_sem.at[q, slot_there],
            device_id=(self.me, self.slab) if toward is None else (self.owners[toward], self.slab),
            device_id_type=pl.DeviceIdType.MESH,
        )

    def arrived(self, q, slot):
        pltpu.make_async_remote_copy(
            src_ref=self.block(q, self.owners[slot]),
            dst_ref=self.block(q, self.owners[slot]),
            send_sem=self.send_sem.at[q, slot],
            recv_sem=self.recv_sem.at[q, slot],
            device_id=(self.owners[1], self.slab),
            device_id_type=pl.DeviceIdType.MESH,
        ).wait_recv()

    def halo_copy(self, slot, up):
        mine, theirs = (self.size_x, 0) if up else (1, self.size_x + 1)
        return pltpu.make_async_remote_copy(
            src_ref=self.block(mine, self.owners[slot]),
            dst_ref=self.block(theirs, self.owners[slot]),
            send_sem=self.halo_send.at[int(up), slot],
            recv_sem=self.halo_recv.at[int(up), slot],
            device_id=(self.me, self.slab + 1 if up else self.slab - 1),
            device_id_type=pl.DeviceIdType.MESH,
        )

    def halo_pass(self, q, slot):
        if q == self.size_x:

            @pl.when(self.has_hi)
            def _():
                self.halo_copy(slot, True).start()

        if q == 1:

            @pl.when(self.has_lo)
            def _():
                self.halo_copy(slot, False).start()

    def local_copy(self, q, y):
        rows = pl.ds(pl.multiple_of(q * self.chans + self.me * self.part, self.part), self.part)
        lanes = pl.ds(pl.multiple_of((y + 1) * self.size_z, self.size_z), self.size_z)
        return pltpu.make_async_copy(
            self.source.at[q - 1, y], self.planes.at[rows, lanes], self.local_sem.at[q]
        )

    def begin(self):
        for q in self.order:

            def put(y, _, q=q):
                self.local_copy(q, y).start()
                return 0

            lax.fori_loop(0, self.size_y, put, 0)
        barrier = pltpu.get_barrier_semaphore()
        for slot in range(1, self.peers):
            pl.semaphore_signal(
                barrier, inc=1, device_id=(self.owners[slot], self.slab), device_id_type=pl.DeviceIdType.MESH
            )
        for step in (1, self.slabs - 1):
            beside = (self.slab + step) % self.slabs
            pl.semaphore_signal(
                barrier, inc=1, device_id=(self.me, beside), device_id_type=pl.DeviceIdType.MESH
            )

        edge = jnp.zeros((self.planes.shape[0], self.size_z), BF16)
        self.planes[:, 0 : self.size_z] = edge
        self.planes[:, (self.size_y + 1) * self.size_z : (self.size_y + 2) * self.size_z] = edge
        cells = slice(self.size_z, (self.size_y + 1) * self.size_z)
        blank = jnp.zeros((self.chans, self.size_y * self.size_z), BF16)

        @pl.when(jnp.logical_not(self.has_lo))
        def _():
            self.planes[0 : self.chans, cells] = blank

        @pl.when(jnp.logical_not(self.has_hi))
        def _():
            self.planes[(self.size_x + 1) * self.chans : (self.size_x + 2) * self.chans, cells] = blank

        pl.semaphore_wait(barrier, self.peers + 1)

        for q in self.order:

            def done(y, _, q=q):
                self.local_copy(q, y).wait()
                return 0

            lax.fori_loop(0, self.size_y, done, 0)
        for stage in range(min(2, len(self.order))):
            self.send_own(stage)

    def send_own(self, stage):
        q = self.order[stage]
        for slot in self.near:
            self.chan_copy(q, 0, slot, self.back(slot)).start()
        self.halo_pass(q, 0)

    def relay(self, stage, q, slot):
        return self.peers == 4 and slot == (1 if stage % 2 else 2)

    def take_near(self, stage):
        q = self.order[stage]
        for slot in self.near:
            self.arrived(q, slot)
            if self.relay(stage, q, slot):
                self.chan_copy(q, slot, 3 - slot, 3).start()
            self.halo_pass(q, slot)
        if stage + 2 < len(self.order):
            self.send_own(stage + 2)

    def take_far(self, stage):
        q = self.order[stage]
        if self.peers == 4:
            self.arrived(q, 3)
            self.halo_pass(q, 3)

    def take_halo(self, up):
        @pl.when(self.has_lo if up else self.has_hi)
        def _():
            for slot in range(self.peers):
                mine, theirs = (self.size_x, 0) if up else (1, self.size_x + 1)
                pltpu.make_async_remote_copy(
                    src_ref=self.block(mine, self.owners[slot]),
                    dst_ref=self.block(theirs, self.owners[slot]),
                    send_sem=self.halo_send.at[int(up), slot],
                    recv_sem=self.halo_recv.at[int(up), slot],
                    device_id=(self.me, self.slab - 1 if up else self.slab + 1),
                    device_id_type=pl.DeviceIdType.MESH,
                ).wait_recv()

    def finish(self):
        for stage, q in enumerate(self.order):
            for slot in self.near:
                self.chan_copy(q, 0, slot, self.back(slot)).wait_send()
                if self.relay(stage, q, slot):
                    self.chan_copy(q, slot, 3 - slot, 3).wait_send()
        for up, there in ((True, self.has_hi), (False, self.has_lo)):

            @pl.when(there)
            def _(up=up):
                for slot in range(self.peers):
                    self.halo_copy(slot, up).wait_send()


def add_plane(planes, w_ref, acc, q, started, chans, size_y, size_z):
    size_x, rows, _ = acc.shape
    taps = [dx for dx in range(3) if 0 <= q - dx < size_x]
    first, last = taps[0], taps[-1] + 1
    count = 2

    def step(index, _):
        y = index * count
        total = None
        for dy in range(3):
            lanes = pl.ds(pl.multiple_of((y + dy) * size_z, size_z), count * size_z)
            part = jnp.dot(
                w_ref[first:last, dy].reshape((last - first) * rows, chans),
                planes[q * chans : (q + 1) * chans, lanes],
                preferred_element_type=F32,
            )
            total = part if total is None else total + part
        lanes = pl.ds(pl.multiple_of(y * size_z, size_z), count * size_z)
        for dx in taps:
            part = total[(dx - first) * rows : (dx - first + 1) * rows]
            if q - dx in started:
                acc[q - dx, :, lanes] += part
            else:
                acc[q - dx, :, lanes] = part
        return 0

    lax.fori_loop(0, size_y // count, step, 0)
    started.update(q - dx for dx in taps)


def tap_sum(acc, x, outs, lanes):
    return (
        acc[x, outs : 2 * outs, lanes]
        + shifted(acc[x, 0:outs, lanes], 1)
        + shifted(acc[x, 2 * outs : 3 * outs, lanes], -1)
    )


def conv(gather, w_ref, acc, finish_plane, aside):
    size_x, chans, size_y, size_z = gather.size_x, gather.chans, gather.size_y, gather.size_z
    started, count, left = set(), {x: 3 for x in range(size_x)}, list(aside)

    def plane(q):
        add_plane(gather.planes, w_ref, acc, q, started, chans, size_y, size_z)
        for dx in range(3):
            if q - dx in count:
                count[q - dx] -= 1
                if count[q - dx] == 0:
                    finish_plane(q - dx)

    gather.begin()
    stages = len(gather.order)
    for stage in range(stages):
        if left:
            left.pop(0)()
        gather.take_near(stage)
        if stage:
            gather.take_far(stage - 1)
            plane(gather.order[stage - 1])
    gather.take_halo(True)
    plane(0)
    gather.take_halo(False)
    plane(size_x + 1)
    gather.take_far(stages - 1)
    plane(gather.order[-1])
    gather.finish()


def forward_kernel(peers, vol_ref, w_ref, bias_ref, cot_ref, out_ref, grad_ref, sum_ref, planes, acc, three, *sems):
    gather = Gather(vol_ref, planes, *sems, peers)
    size_x, size_y, outs, size_z = cot_ref.shape

    def finish_plane(x):
        def step(y, _):
            lanes = pl.ds(pl.multiple_of(y * size_z, size_z), size_z)
            pre = tap_sum(acc, x, outs, lanes) + bias_ref[...]
            sig = jax.nn.sigmoid(pre)
            out_ref[x, y] = (pre * sig).astype(BF16)
            grad = cot_ref[x, y].astype(F32) * sig * (1.0 + pre * (1.0 - sig))
            held = grad.astype(BF16)
            grad_ref[x, y] = held
            grad = held.astype(F32)
            three[x, 0:outs, lanes] = shifted(grad, -1).astype(BF16)
            three[x, outs : 2 * outs, lanes] = held
            three[x, 2 * outs : 3 * outs, lanes] = shifted(grad, 1).astype(BF16)
            return 0

        lax.fori_loop(0, size_y, step, 0)

    conv(gather, w_ref, acc, finish_plane, ())
    sum_ref[...] = jnp.zeros_like(sum_ref)
    chans, cells = gather.chans, size_y * size_z

    def step(x, _):
        for dy in range(3):
            cube = planes[pl.ds(pl.multiple_of(x * chans, chans), 3 * chans), dy * size_z : dy * size_z + cells]
            part = lax.dot_general(
                three[x], cube, (((1,), (1,)), ((), ())), preferred_element_type=F32
            )
            for dx in range(3):
                sum_ref[dx, dy] += part[:, dx * chans : (dx + 1) * chans]
        return 0

    lax.fori_loop(0, size_x, step, 0)
    sum_ref[...] = sum_ref[...] * (1.0 / math.sqrt(size_x * cells * gather.slabs))


def input_kernel(peers, grad_ref, pieces_ref, out_ref, planes, acc, w_ref, *sems):
    gather = Gather(grad_ref, planes, *sems, peers)
    size_x, size_y, outs, size_z = out_ref.shape

    def turn():
        def step(tap, _):
            dx, dy, dz = tap // 9, tap // 3 % 3, tap % 3
            whole = jnp.concatenate([pieces_ref[i, 26 - tap] for i in range(peers)], axis=0)
            rows = pl.ds(pl.multiple_of(dz * outs, outs), outs)
            w_ref[dx, dy, rows] = whole.astype(F32).T.astype(BF16)
            return 0

        lax.fori_loop(0, 27, step, 0)

    def finish_plane(x):
        def step(y, _):
            lanes = pl.ds(pl.multiple_of(y * size_z, size_z), size_z)
            out_ref[x, y] = tap_sum(acc, x, outs, lanes).astype(BF16)
            return 0

        lax.fori_loop(0, size_y, step, 0)

    conv(gather, w_ref, acc, finish_plane, (turn,))


def call(kernel, args, outs, extra, rows, flops, identity):
    whole = pl.BlockSpec(memory_space=pltpu.VMEM)
    peers = lax.axis_size("chan")
    size_x, size_y, part, size_z = args[0].shape
    planes = size_x + 2
    size = sum(a.size * a.dtype.itemsize for a in args)
    return pl.pallas_call(
        functools.partial(kernel, peers),
        out_shape=outs,
        in_specs=[pl.BlockSpec(memory_space=pl.ANY)] + [whole] * (len(args) - 1),
        out_specs=jax.tree.map(lambda _: whole, outs),
        scratch_shapes=[
            pltpu.VMEM((planes * part * peers, (size_y + 2) * size_z), BF16),
            pltpu.VMEM((size_x, rows, size_y * size_z), F32),
            *extra,
            pltpu.SemaphoreType.DMA((planes,)),
            pltpu.SemaphoreType.DMA((planes, peers)),
            pltpu.SemaphoreType.DMA((planes, peers)),
            pltpu.SemaphoreType.DMA((2, peers)),
            pltpu.SemaphoreType.DMA((2, peers)),
        ],
        compiler_params=pltpu.CompilerParams(
            vmem_limit_bytes=VMEM_LIMIT, collective_id=identity, has_side_effects=True
        ),
        cost_estimate=pl.CostEstimate(flops=flops, bytes_accessed=size, transcendentals=0),
    )(*args)


def on_device(volume, kernel, bias, cotangent):
    size_x, size_y, chans_local, size_z = volume.shape
    taps, outs, chans = kernel.shape
    shape = jax.ShapeDtypeStruct
    flops = 2 * size_x * size_y * size_z * taps * outs * chans
    w_forward = kernel.reshape(3, 3, 3 * outs, chans)
    peers = lax.axis_size("chan")
    ins, all_outs = chans // peers, outs * peers
    pieces = kernel.reshape(taps, outs, peers, ins).transpose(2, 0, 1, 3)
    pieces = lax.all_to_all(pieces, "chan", split_axis=0, concat_axis=0, tiled=True)
    column = jnp.broadcast_to(bias.reshape(outs, 1), (outs, size_z))

    output, grad_pre, partial = call(
        forward_kernel,
        (volume, w_forward, column, cotangent),
        (
            shape(cotangent.shape, BF16),
            shape(cotangent.shape, BF16),
            shape((3, 3, 3 * outs, chans), F32),
        ),
        [pltpu.VMEM((size_x, 3 * outs, size_y * size_z), BF16)],
        3 * outs,
        2 * flops,
        0,
    )
    weight_grad = lax.psum(partial, "space").reshape(taps, outs, chans)
    input_grad = call(
        input_kernel,
        (grad_pre, pieces),
        shape(volume.shape, BF16),
        [pltpu.VMEM((3, 3, 3 * ins, all_outs), BF16)],
        3 * ins,
        flops,
        1,
    )
    return output, input_grad, weight_grad


def solution(mesh):
    return jax.shard_map(
        on_device,
        mesh=mesh,
        in_specs=(
            P("space", None, "chan", None),
            P(None, "chan", None),
            P("chan"),
            P("space", None, "chan", None),
        ),
        out_specs=(
            P("space", None, "chan", None),
            P("space", None, "chan", None),
            P(None, "chan", None),
        ),
        check_vma=False,
    )
```
